32 devices in a mesh: rows: 4 (over y, x), chan: 8 (over z, core).
Axes of the slice: x: 2, y: 2, z: 4, core: 2. Of those that a mesh axis runs over, the one named last changes fastest.
Arguments:
- tokens: bfloat16 [8, 2048, 768], P('rows', 'chan'), may hold values from -6 to 6
- lengths: int32 [8, 4], P('rows'), may hold values from 1 to 1024, 2048 in all within a row
- norm1_gain: float32 [768], replicated, may hold values from 0.5 to 1.5
- norm1_bias: float32 [768], replicated, may hold values from -1.5 to 1.5
- query_weight: bfloat16 [768, 768], replicated, may hold values from -0.21875 to 0.21875
- query_offset_bias: float32 [768], replicated, may hold values from -4 to 4
- key_weight: bfloat16 [768, 768], replicated, may hold values from -0.21875 to 0.21875
- value_weight: bfloat16 [768, 768], replicated, may hold values from -0.21875 to 0.21875
- value_offset_bias: float32 [768], replicated, may hold values from -1.5 to 1.5
- output_weight: bfloat16 [768, 768], replicated, may hold values from -1.75 to 1.75
- output_bias: float32 [768], replicated, may hold values from -1.5 to 1.5
- norm2_gain: float32 [768], replicated, may hold values from 0.5 to 1.5
- norm2_bias: float32 [768], replicated, may hold values from -1.5 to 1.5
- raising_weight: bfloat16 [768, 3072], replicated, may hold values from -0.21875 to 0.21875
- raising_bias: float32 [3072], replicated, may hold values from -2.5 to 2.5
- lowering_weight: bfloat16 [3072, 768], replicated, may hold values from -0.109375 to 0.109375
- lowering_bias: float32 [768], replicated, may hold values from -1.5 to 1.5
- pair_bias: float32 [1024, 1024], replicated, may hold values from -4 to 4
- out_cotangent: bfloat16 [8, 2048, 768], P('rows', 'chan'), may hold values from -6 to 6
Outputs:
- block_out: bfloat16 [8, 2048, 768], P('rows', 'chan')
- input_grad: float32 [8, 2048, 768], P('rows', 'chan')
- norm1_gain_grad: float32 [768], P('chan')
- norm1_bias_grad: float32 [768], P('chan')
- w_query_grad: float32 [768, 768], P('chan')
- query_bias_grad: float32 [768], P('chan')
- w_key_grad: float32 [768, 768], P('chan')
- w_value_grad: float32 [768, 768], P('chan')
- value_bias_grad: float32 [768], P('chan')
- w_out_grad: float32 [768, 768], P('chan')
- out_bias_grad: float32 [768], P('chan')
- norm2_gain_grad: float32 [768], P('chan')
- norm2_bias_grad: float32 [768], P('chan')
- w_up_grad: float32 [768, 3072], P('chan')
- up_bias_grad: float32 [3072], P('chan')
- w_down_grad: float32 [3072, 768], P('chan')
- down_bias_grad: float32 [768], P('chan')
- pair_bias_grad: float32 [1024, 1024], P('chan')
The draws below stay inside these ranges and needn't reach their ends.
Inputs may be any that keep to these rules, and one draw needn't show every extreme that they name: Each row holds 4 documents whose lengths sum to 2048; in every row the longest has exactly 1024 tokens.
All inputs are finite; a program needn't handle non-finite values.
Results may differ from the reference program's by a relative error of at most 0.012.
Values may be sent and summed in bfloat16 or wider, within the bound.
No kernel may reach another device: no remote copies, remote signals or barrier semaphores. Data moves between devices by JAX's collectives and lax.ppermute only.
A program may use at most 192 MiB of HBM per device.

```python
import math
import jax
import jax.numpy as jnp
import numpy as np
from jax import lax

D = 768
FF = 3072
L = 2048
WIN = 256
MAXDOC = 1024
NDOC = 4
NSEQ = 8


def block_scale(key, extent, cuts, smallest, high):
    loudness, own = 1.0, jax.random.fold_in(key, 6)
    for dim, parts in cuts:
        draws = jnp.exp(jax.random.uniform(jax.random.fold_in(own, dim), (parts,), jnp.float32, smallest / len(cuts), high / len(cuts)))
        loudness = loudness * jnp.repeat(draws, extent[dim] // parts).reshape([-1 if axis == dim else 1 for axis in range(len(extent))])
    return loudness


def profile(number_of, total, reach, skew):
    loads = [(1 << 20) // math.isqrt(rank ** skew) + 1 for rank in range(2, number_of + 1)]
    surplus, given = total - reach - (number_of - 1), [1] * (number_of - 1)
    while surplus > 0:
        movable = [i for i in range(number_of - 1) if given[i] < reach]
        whole, left = sum([loads[i] for i in movable]), surplus
        for i in movable:
            addition = min(reach - given[i], max(1, left * loads[i] // whole), surplus)
            given[i] = given[i] + addition
            surplus = surplus - addition
    return np.array([reach] + given)


def ragged(own_key, amount, total, limit, slope):
    if amount == 2:
        one = jax.random.randint(own_key, (), max(1, total - limit), min(limit, total - 1) + 1)
        return jnp.stack([one, total - one])
    tallies = jnp.asarray(profile(amount, total, limit, slope), jnp.int32)
    couples = (amount - 1) // 2
    donor, taker = tallies[1:1 + 2 * couples:2], tallies[2:2 + 2 * couples:2]
    room = jnp.minimum(donor - 1, limit - taker)
    shifted = jax.random.randint(jax.random.fold_in(own_key, 1), (couples,), 0, 1 << 20) % (room + 1)
    tallies = tallies.at[1:1 + 2 * couples:2].set(donor - shifted).at[2:2 + 2 * couples:2].set(taker + shifted)
    return tallies[jax.random.permutation(jax.random.fold_in(own_key, 2), amount)]


def noise(own_key, extent, scale, limit, pieces=(), held_as=jnp.bfloat16):
    factor_of = block_scale(own_key, extent, pieces, -0.22, 0.18) if pieces else 1.0
    drawn = jax.random.normal(own_key, extent, jnp.float32) * scale * factor_of
    return jnp.minimum(jnp.maximum(drawn, -limit), limit).astype(held_as)


def setup_inputs(seed: int = 0) -> dict:
    splits = jax.random.split(jax.random.key(seed), 20)
    tokens = noise(splits[0], (NSEQ, L, D), 1.0, 6.0, ((0, 4), (1, 8)))
    lengths = jax.vmap(lambda own: ragged(own, NDOC, L, MAXDOC, 2))(jax.random.split(splits[1], NSEQ)).reshape((NSEQ, NDOC)).astype(jnp.int32)
    norm1_gain = jnp.clip(1.0 + 0.1 * jax.random.normal(splits[2], (D,), jnp.float32), 0.5, 1.5)
    norm1_bias = noise(splits[3], (D,), 0.3, 1.5, (), jnp.float32)
    query_weight = noise(splits[4], (D, D), D ** -0.5, 0.21875)
    query_offset_bias = noise(splits[5], (D,), 1.0, 4.0, (), jnp.float32)
    key_weight = noise(splits[6], (D, D), D ** -0.5, 0.21875)
    value_weight = noise(splits[7], (D, D), D ** -0.5, 0.21875)
    value_offset_bias = noise(splits[8], (D,), 0.3, 1.5, (), jnp.float32)
    output_weight = noise(splits[9], (D, D), (D // 64) ** -0.5, 1.75)
    output_bias = noise(splits[10], (D,), 0.3, 1.5, (), jnp.float32)
    norm2_gain = jnp.clip(1.0 + 0.1 * jax.random.normal(splits[11], (D,), jnp.float32), 0.5, 1.5)
    norm2_bias = noise(splits[12], (D,), 0.3, 1.5, (), jnp.float32)
    raising_weight = noise(splits[13], (D, FF), D ** -0.5, 0.21875)
    raising_bias = noise(splits[14], (FF,), 0.5, 2.5, (), jnp.float32)
    lowering_weight = noise(splits[15], (FF, D), FF ** -0.5, 0.109375)
    lowering_bias = noise(splits[16], (D,), 0.3, 1.5, (), jnp.float32)
    pair_bias = noise(splits[17], (MAXDOC, MAXDOC), 1.0, 4.0, (), jnp.float32)
    out_cotangent = noise(splits[18], (NSEQ, L, D), 1.0, 6.0, ((0, 4), (1, 8)))
    return {"tokens": tokens, "lengths": lengths, "norm1_gain": norm1_gain, "norm1_bias": norm1_bias, "query_weight": query_weight, "query_offset_bias": query_offset_bias, "key_weight": key_weight, "value_weight": value_weight, "value_offset_bias": value_offset_bias, "output_weight": output_weight, "output_bias": output_bias, "norm2_gain": norm2_gain, "norm2_bias": norm2_bias, "raising_weight": raising_weight, "raising_bias": raising_bias, "lowering_weight": lowering_weight, "lowering_bias": lowering_bias, "pair_bias": pair_bias, "out_cotangent": out_cotangent}


EPSILON = 1e-05
FULL_ACCURACY = lax.Precision.HIGHEST

@jax.custom_vjp
def reduced_copy(v):
    return lax.optimization_barrier(v.astype(jnp.bfloat16)).astype(jnp.float32)

@jax.custom_vjp
def reduced_return(v):
    return v

def low_keep(v):
    return (reduced_copy(v), None)

def low_pass(kept, grad):
    return (grad,)

def back_keep(v):
    return (v, None)

def back_low(kept, grad):
    return (reduced_copy(grad),)
reduced_copy.defvjp(low_keep, low_pass)
reduced_return.defvjp(back_keep, back_low)

def layer_norm(hidden, norm_gain, norm_shift):
    average = lax.optimization_barrier(jnp.mean(hidden, axis=-1, keepdims=True))
    centered = hidden - average
    spread = lax.optimization_barrier(jnp.mean(centered * centered, axis=-1, keepdims=True))
    return centered * lax.rsqrt(spread + EPSILON) * norm_gain + norm_shift

def doc_layout(row_lengths, length):
    places = jnp.arange(length, dtype=jnp.int32)
    doc_ends = jnp.cumsum(row_lengths).astype(jnp.int32)
    doc_starts = (doc_ends - row_lengths).astype(jnp.int32)
    doc_index = lax.optimization_barrier(jnp.sum((places[:, None] >= doc_ends[None, :]).astype(jnp.int32), axis=1)).astype(jnp.int32)
    chosen = doc_index[:, None] == jnp.arange(row_lengths.shape[0], dtype=jnp.int32)[None, :]
    offsets = lax.optimization_barrier(jnp.sum(jnp.where(chosen, doc_starts[None, :], 0), axis=1)).astype(jnp.int32)
    return (places, doc_index, (places - offsets).astype(jnp.int32))

def pair_weights(row_lengths, pair_bias, length):
    places, doc_index, positions = doc_layout(row_lengths, length)
    near = (doc_index[:, None] == doc_index[None, :]) & (jnp.abs(places[:, None] - places[None, :]) < WIN)
    return jnp.where(near, jnp.exp(pair_bias[positions[:, None], positions[None, :]]), 0.0)

def mix_row(query_rows, projected_keys, projected_values, row_lengths, pair_bias):
    weights = reduced_copy(pair_weights(row_lengths, pair_bias, query_rows.shape[0]))
    exp_key = jnp.exp(projected_keys)
    carried = reduced_copy(exp_key * projected_values)
    exp_low = reduced_copy(exp_key)
    numerator = reduced_return(jnp.dot(weights, carried, precision=FULL_ACCURACY))
    denominator = reduced_return(jnp.dot(weights, exp_low, precision=FULL_ACCURACY))
    return reduced_copy(reduced_return(jax.nn.sigmoid(query_rows) * numerator / denominator))

def forward(token_values, lengths, norm1_gain, norm1_bias, query_weight, query_offset_bias, key_weight, value_weight, value_offset_bias, output_weight, output_bias, norm2_gain, norm2_bias, raising_weight, raising_bias, lowering_weight, lowering_bias, pair_bias):
    entry_normalized = reduced_copy(layer_norm(token_values, norm1_gain, norm1_bias))
    query_matrix = reduced_copy(reduced_return(jnp.einsum('rju,uq->rjq', entry_normalized, query_weight, precision=FULL_ACCURACY) + query_offset_bias))
    projected_keys = reduced_copy(reduced_return(jnp.einsum('rju,uq->rjq', entry_normalized, key_weight, precision=FULL_ACCURACY)))
    projected_values = reduced_copy(reduced_return(jnp.einsum('rju,uq->rjq', entry_normalized, value_weight, precision=FULL_ACCURACY) + value_offset_bias))

    def one_row(inputs):
        return mix_row(inputs[0], inputs[1], inputs[2], inputs[3], pair_bias)
    mixed_output = lax.map(jax.checkpoint(one_row), (query_matrix, projected_keys, projected_values, lengths))
    attended_rows = reduced_return(jnp.einsum('rju,uq->rjq', mixed_output, output_weight, precision=FULL_ACCURACY) + output_bias)
    residual_stream = token_values + attended_rows
    middle_normalized = reduced_copy(layer_norm(residual_stream, norm2_gain, norm2_bias))
    upward_hidden = reduced_return(jnp.einsum('pic,cw->piw', middle_normalized, raising_weight, precision=FULL_ACCURACY) + raising_bias)
    active_hidden = reduced_copy(jax.nn.gelu(upward_hidden, approximate=True))
    return residual_stream + jnp.einsum('exp,pj->exj', active_hidden, lowering_weight, precision=FULL_ACCURACY) + lowering_bias

def reference(tokens, lengths, norm1_gain, norm1_bias, query_weight, query_offset_bias, key_weight, value_weight, value_offset_bias, output_weight, output_bias, norm2_gain, norm2_bias, raising_weight, raising_bias, lowering_weight, lowering_bias, pair_bias, out_cotangent):

    def wrapped(*floats):
        return forward(floats[0], lengths, *floats[1:])
    result, pullback = jax.vjp(wrapped, tokens.astype(jnp.float32), norm1_gain, norm1_bias, query_weight.astype(jnp.float32), query_offset_bias, key_weight.astype(jnp.float32), value_weight.astype(jnp.float32), value_offset_bias, output_weight.astype(jnp.float32), output_bias, norm2_gain, norm2_bias, raising_weight.astype(jnp.float32), raising_bias, lowering_weight.astype(jnp.float32), lowering_bias, pair_bias)
    input_grad, norm1_gain_grad, norm1_bias_grad, w_query_grad, query_bias_grad, w_key_grad, w_value_grad, value_bias_grad, w_out_grad, out_bias_grad, norm2_gain_grad, norm2_bias_grad, w_up_grad, up_bias_grad, w_down_grad, down_bias_grad, pair_bias_grad = pullback(out_cotangent.astype(jnp.float32))
    return (result.astype(jnp.bfloat16), input_grad, norm1_gain_grad, norm1_bias_grad, w_query_grad, query_bias_grad, w_key_grad, w_value_grad, value_bias_grad, w_out_grad, out_bias_grad, norm2_gain_grad, norm2_bias_grad, w_up_grad, up_bias_grad, w_down_grad, down_bias_grad, pair_bias_grad)
```

```python
from functools import partial

import jax
import jax.numpy as jnp
from jax import lax
from jax.experimental import pallas as pl
from jax.experimental.pallas import tpu as pltpu
from jax.sharding import PartitionSpec as P

WIN = 256
MAXDOC = 1024
EPSILON = 1e-05
BAND = 640
F32 = jnp.float32
BF16 = jnp.bfloat16
GELU_A = 0.7978845608
GELU_B = 0.044715


def up_to(n, k):
    return -(-n // k) * k


def params(mib):
    return pltpu.CompilerParams(vmem_limit_bytes=mib << 20)


def cost(flops, nbytes):
    return pl.CostEstimate(flops=int(flops), bytes_accessed=int(nbytes), transcendentals=0)


def dot_nn(a, b):
    return lax.dot_general(a, b, (((1,), (0,)), ((), ())), preferred_element_type=F32)


def dot_nt(a, b):
    return lax.dot_general(a, b, (((1,), (1,)), ((), ())), preferred_element_type=F32)


def dot_tn(a, b):
    return lax.dot_general(a, b, (((0,), (0,)), ((), ())), preferred_element_type=F32)


def tiles(count, size, step):
    def one(i, carry):
        step(pl.multiple_of(i * size, size))
        return carry

    lax.fori_loop(0, count // size, one, 0)


def normalize(hidden):
    average = jnp.mean(hidden, axis=-1, keepdims=True)
    centered = hidden - average
    spread = jnp.mean(centered * centered, axis=-1, keepdims=True)
    inverse = lax.rsqrt(spread + EPSILON)
    return centered * inverse, inverse


def norm_pull(grad_out, normed, inverse, gain):
    scaled = grad_out * gain
    mean_scaled = jnp.mean(scaled, axis=-1, keepdims=True)
    mean_cross = jnp.mean(scaled * normed, axis=-1, keepdims=True)
    return inverse * (scaled - mean_scaled - normed * mean_cross)


def whole(shape):
    zeros = (0,) * len(shape)
    return pl.BlockSpec(shape, lambda *_: zeros)


def weights_kernel(geom, t0_ref, len_ref, pb_hbm, wl, wo, wr, w2l, w2r, pb, sem):
    rows, blk, halo, docs, padr, padc = geom
    copy = pltpu.make_async_copy(
        pb_hbm, pb.at[pl.ds(padr, MAXDOC), pl.ds(padc, MAXDOC)], sem
    )
    copy.start()
    for ref in (wl, wo, wr, w2l, w2r):
        ref[...] = jnp.zeros_like(ref)
    copy.wait()
    t0 = t0_ref[0]
    size = 32

    def fill(out, first, last, t_first, t_count, u_first, u_count):
        low = jnp.clip(first - t_first, 0, t_count)
        high = jnp.clip(last - t_first, 0, t_count)
        wide = up_to(u_count, 128) + 128
        col = padc + u_first - first
        col_base = pl.multiple_of((col // 128) * 128, 128)
        row = padr + t_first - first
        row_base = (row // 8) * 8
        u = u_first + lax.broadcasted_iota(jnp.int32, (size, u_count), 1)
        u_inside = (u >= first) & (u < last)

        def step(c, carry):
            i0 = pl.multiple_of(c * size, size)
            x = pb[pl.ds(pl.multiple_of(row_base + i0, 8), size + 8), pl.ds(col_base, wide)]
            x = pltpu.roll(x, size + 8 - (row - row_base), 0)[:size]
            x = pltpu.roll(x, wide - (col - col_base), 1)[:, :u_count]
            t = t_first + i0 + lax.broadcasted_iota(jnp.int32, (size, u_count), 0)
            valid = u_inside & (t >= first) & (t < last) & (jnp.abs(t - u) < WIN)
            out[pl.ds(i0, size), :] = jnp.where(valid, jnp.exp(x), out[pl.ds(i0, size), :])
            return carry

        lax.fori_loop(low // size, (high + size - 1) // size, step, 0)

    def one_row(r, carry):
        def one_doc(d, first):
            last = first + len_ref[r, d]

            @pl.when((first < t0 + blk) & (last > t0))
            def _():
                fill(wl.at[r], first, last, t0, blk, t0 - halo, halo)
                fill(wo.at[r], first, last, t0, blk, t0, blk)
                fill(wr.at[r], first, last, t0, blk, t0 + blk, halo)
                fill(w2l.at[r], first, last, t0 - halo, halo, t0, blk)
                fill(w2r.at[r], first, last, t0 + blk, halo, t0, blk)

            return last

        lax.fori_loop(0, docs, one_doc, jnp.int32(0))
        return carry

    lax.fori_loop(0, rows, one_row, 0)


def pair_weights(t0, lengths, pair_bias, blk, halo):
    rows, docs = lengths.shape
    padr, padc = up_to(blk + halo, 8), up_to(blk + halo, 128)
    shapes = [(blk, halo), (blk, blk), (blk, halo), (halo, blk), (halo, blk)]
    return pl.pallas_call(
        partial(weights_kernel, (rows, blk, halo, docs, padr, padc)),
        out_shape=[jax.ShapeDtypeStruct((rows,) + s, F32) for s in shapes],
        in_specs=[
            pl.BlockSpec(memory_space=pltpu.SMEM),
            pl.BlockSpec(memory_space=pltpu.SMEM),
            pl.BlockSpec(memory_space=pl.ANY),
        ],
        scratch_shapes=[
            pltpu.VMEM((2 * padr + MAXDOC + 40, 2 * padc + MAXDOC + 128), F32),
            pltpu.SemaphoreType.DMA,
        ],
        compiler_params=params(48),
        cost_estimate=cost(1e9, 12e6),
        name="weights",
    )(t0, lengths, pair_bias)


def project_kernel(own, *refs):
    if own:
        x, gain, bias, wq, bq, wk, wv, bv, normed, q, k, v, ce = refs
    else:
        x, gain, bias, wk, wv, bv, ce, normed = refs
    count, d = x.shape
    sub = min(32, count)

    def norm_tile(i):
        unit, _ = normalize(x[pl.ds(i, sub), :].astype(F32))
        normed[pl.ds(i, sub), :] = (unit * gain[...] + bias[...]).astype(BF16)

    tiles(count, sub, norm_tile)
    low = normed[...]
    for n in range(0, d, 256):
        c = slice(n, n + 256)
        if own:
            q[:, c] = (dot_nn(low, wq[:, c]) + bq[:, c]).astype(BF16)
        key = dot_nn(low, wk[:, c]).astype(BF16)
        value = (dot_nn(low, wv[:, c]) + bv[:, c]).astype(BF16)
        if own:
            k[:, c] = key
            v[:, c] = value
        exp_key = jnp.exp(key.astype(F32))
        ce[:, c] = (exp_key * value.astype(F32)).astype(BF16)
        ce[:, slice(d + n, d + n + 256)] = exp_key.astype(BF16)


def project(x, gain, bias, wq, bq, wk, wv, bv, own):
    t, d = x.shape
    tm = min(256, t)
    row = lambda c: pl.BlockSpec((tm, c), lambda i: (i, 0))
    vec, mat = whole((1, d)), whole((d, d))
    out = lambda c: jax.ShapeDtypeStruct((t, c), BF16)
    if own:
        return pl.pallas_call(
            partial(project_kernel, True),
            grid=(t // tm,),
            out_shape=[out(d)] * 4 + [out(2 * d)],
            in_specs=[row(d), vec, vec, mat, vec, mat, mat, vec],
            out_specs=[row(d)] * 4 + [row(2 * d)],
            compiler_params=params(40),
            cost_estimate=cost(6 * t * d * d, 20 * t * d),
            name="project_own",
        )(x, gain, bias, wq, bq, wk, wv, bv)
    return pl.pallas_call(
        partial(project_kernel, False),
        grid=(t // tm,),
        out_shape=out(2 * d),
        in_specs=[row(d), vec, vec, mat, mat, vec],
        out_specs=row(2 * d),
        scratch_shapes=[pltpu.VMEM((tm, d), BF16)],
        compiler_params=params(40),
        cost_estimate=cost(4 * t * d * d, 10 * t * d),
        name="project_halo",
    )(x, gain, bias, wk, wv, bv)


def mix_kernel(
    wl, wo, wr, cl, co, cr, q, x, w_out, b_out, gain, bias,
    mixed, ratio, den, resid, mid, acc,
):
    count, d = q.shape
    sub = min(32, count)
    low = [w[...].astype(BF16) for w in (wl, wo, wr)]
    for n in range(0, d, 256):
        c, e = slice(n, n + 256), slice(d + n, d + n + 256)
        num = sum(dot_nn(w, k[:, c]) for w, k in zip(low, (cl, co, cr)))
        below = sum(dot_nn(w, k[:, e]) for w, k in zip(low, (cl, co, cr)))
        quotient = num / below
        ratio[:, c] = quotient
        den[:, c] = below
        mixed[:, c] = (jax.nn.sigmoid(q[:, c].astype(F32)) * quotient).astype(BF16)
    rows = mixed[...]
    for n in range(0, d, 256):
        c = slice(n, n + 256)
        acc[:, c] = dot_nn(rows, w_out[:, c])

    def norm_tile(i):
        at = pl.ds(i, sub)
        stream = x[at, :].astype(F32) + acc[at, :] + b_out[...]
        resid[at, :] = stream
        unit, _ = normalize(stream)
        mid[at, :] = (unit * gain[...] + bias[...]).astype(BF16)

    tiles(count, sub, norm_tile)


def mix(weights, ce, q, x, w_out, b_out, gain, bias):
    rows, blk, d = q.shape
    halo = ce[0].shape[1]
    blk3 = lambda *s: pl.BlockSpec((None,) + s, lambda r: (r,) + (0,) * len(s))
    vec = whole((1, d))
    out = lambda t: jax.ShapeDtypeStruct((rows, blk, d), t)
    return pl.pallas_call(
        mix_kernel,
        grid=(rows,),
        out_shape=[out(BF16), out(F32), out(F32), out(F32), out(BF16)],
        in_specs=[
            blk3(blk, halo), blk3(blk, blk), blk3(blk, halo),
            blk3(halo, 2 * d), blk3(blk, 2 * d), blk3(halo, 2 * d),
            blk3(blk, d), blk3(blk, d), whole((d, d)), vec, vec, vec,
        ],
        out_specs=[blk3(blk, d)] * 5,
        scratch_shapes=[pltpu.VMEM((blk, d), F32)],
        compiler_params=params(48),
        cost_estimate=cost(4e9, 20e6),
        name="mix",
    )(*weights, *ce, q, x, w_out, b_out, gain, bias)


def feed_kernel(
    mid, cot, resid, w_up, b_up, w_dn, b_dn,
    out, mid_grad, dn_grad, up_grad, up_bias, dn_bias,
    acc, act, ug, mid_t,
):
    step, last = pl.program_id(0), pl.num_programs(0) - 1
    count, d = mid.shape
    fc = w_up.shape[1]
    mt = min(256, count)

    @pl.when(step == 0)
    def _():
        acc[...] = jnp.zeros_like(acc)
        mid_grad[...] = jnp.zeros_like(mid_grad)
        mid_t[...] = mid[...].T
        dn_bias[...] = jnp.sum(cot[...].astype(F32), axis=0, keepdims=True)

    up_bias[...] = jnp.zeros_like(up_bias)

    def hidden(m):
        rows = pl.ds(m, mt)
        a, g = mid[rows, :], cot[rows, :]
        for n in range(0, fc, 256):
            c = slice(n, n + 256)
            z = dot_nn(a, w_up[:, c]) + b_up[:, c]
            ag = dot_nt(g, w_dn[c, :])
            z2 = z * z
            t = jnp.tanh(GELU_A * z * (1.0 + GELU_B * z2))
            half = 0.5 * (1.0 + t)
            act[rows, c] = (z * half).astype(BF16)
            slope = half + (0.5 * GELU_A) * z * (1.0 - t * t) * (1.0 + (3.0 * GELU_B) * z2)
            low = (ag * slope).astype(BF16)
            ug[rows, c] = low
            up_bias[:, c] += jnp.sum(low.astype(F32), axis=0, keepdims=True)

    tiles(count, mt, hidden)

    def pulls(m):
        rows = pl.ds(m, mt)
        a, g = act[rows, :], ug[rows, :]
        for n in range(0, d, 256):
            c = slice(n, n + 256)
            acc[rows, c] += dot_nn(a, w_dn[:, c])
            mid_grad[rows, c] += dot_nt(g, w_up[c, :])

    tiles(count, mt, pulls)
    for k in range(0, fc, 256):
        c = slice(k, k + 256)
        dn_grad[c, :] = dot_tn(act[:, c], cot[...]).astype(BF16)
    for k in range(0, d, 256):
        c = slice(k, k + 256)
        up_grad[c, :] = dot_nn(mid_t[c, :], ug[...]).astype(BF16)

    @pl.when(step == last)
    def _():
        out[...] = (resid[...] + acc[...] + b_dn[...]).astype(BF16)


def feed(mid, cot, resid, w_up, b_up, w_dn, b_dn):
    t, d = mid.shape
    ff = w_up.shape[1]
    fc = 768
    full = whole((t, d))
    return pl.pallas_call(
        feed_kernel,
        grid=(ff // fc,),
        out_shape=[
            jax.ShapeDtypeStruct((t, d), BF16),
            jax.ShapeDtypeStruct((t, d), F32),
            jax.ShapeDtypeStruct((ff, d), BF16),
            jax.ShapeDtypeStruct((d, ff), BF16),
            jax.ShapeDtypeStruct((1, ff), F32),
            jax.ShapeDtypeStruct((1, d), F32),
        ],
        in_specs=[
            full, full, full,
            pl.BlockSpec((d, fc), lambda f: (0, f)),
            pl.BlockSpec((1, fc), lambda f: (0, f)),
            pl.BlockSpec((fc, d), lambda f: (f, 0)),
            whole((1, d)),
        ],
        out_specs=[
            full, full,
            pl.BlockSpec((fc, d), lambda f: (f, 0)),
            pl.BlockSpec((d, fc), lambda f: (0, f)),
            pl.BlockSpec((1, fc), lambda f: (0, f)),
            whole((1, d)),
        ],
        scratch_shapes=[
            pltpu.VMEM((t, d), F32),
            pltpu.VMEM((t, fc), BF16),
            pltpu.VMEM((t, fc), BF16),
            pltpu.VMEM((d, t), BF16),
        ],
        compiler_params=params(56),
        cost_estimate=cost(12 * t * d * ff, 8 * d * ff),
        name="feed",
    )(mid, cot, resid, w_up, b_up, w_dn, b_dn)


def middle_kernel(
    mid_grad, resid, cot, q, ratio, den, w_out, gain,
    res_grad, res_low, q_grad, pair, vectors,
):
    count, d = q.shape
    sub = min(32, count)

    @pl.when(pl.program_id(0) == 0)
    def _():
        vectors[...] = jnp.zeros_like(vectors)

    def norm_tile(i):
        at = pl.ds(i, sub)
        unit, inverse = normalize(resid[at, :])
        g = mid_grad[at, :]
        total = cot[at, :].astype(F32) + norm_pull(g, unit, inverse, gain[...])
        res_grad[at, :] = total
        low = total.astype(BF16)
        res_low[at, :] = low
        vectors[0:1, :] += jnp.sum(g * unit, axis=0, keepdims=True)
        vectors[1:2, :] += jnp.sum(g, axis=0, keepdims=True)
        vectors[2:3, :] += jnp.sum(low.astype(F32), axis=0, keepdims=True)

    tiles(count, sub, norm_tile)
    low = res_low[...]
    for n in range(0, d, 256):
        c, e = slice(n, n + 256), slice(d + n, d + n + 256)
        grad = dot_nt(low, w_out[c, :]).astype(BF16).astype(F32)
        gate = jax.nn.sigmoid(q[:, c].astype(F32))
        quotient = ratio[:, c]
        through = grad * gate
        over = through / den[:, c]
        back = (through * quotient * (1.0 - gate)).astype(BF16)
        q_grad[:, c] = back
        pair[:, c] = over.astype(BF16)
        pair[:, e] = (-over * quotient).astype(BF16)
        vectors[3:4, c] += jnp.sum(back.astype(F32), axis=0, keepdims=True)


def middle(mid_grad, resid, cot, q, ratio, den, w_out, gain):
    t, d = q.shape
    tm = min(256, t)
    row = lambda c: pl.BlockSpec((tm, c), lambda i: (i, 0))
    return pl.pallas_call(
        middle_kernel,
        grid=(t // tm,),
        out_shape=[
            jax.ShapeDtypeStruct((t, d), F32),
            jax.ShapeDtypeStruct((t, d), BF16),
            jax.ShapeDtypeStruct((t, d), BF16),
            jax.ShapeDtypeStruct((t, 2 * d), BF16),
            jax.ShapeDtypeStruct((8, d), F32),
        ],
        in_specs=[row(d)] * 6 + [whole((d, d)), whole((1, d))],
        out_specs=[row(d), row(d), row(d), row(2 * d), whole((8, d))],
        compiler_params=params(48),
        cost_estimate=cost(2 * t * d * d, 30 * t * d),
        name="middle",
    )(mid_grad, resid, cot, q, ratio, den, w_out, gain)


def outer_kernel(geom, t0_ref, len_ref, wl, wo, wr, g, cl, co, cr, band, acc, piece):
    blk, halo, docs, padr, padc = geom
    r, last_row = pl.program_id(0), pl.num_programs(0) - 1
    t0 = t0_ref[0]
    size = 32

    @pl.when(r == 0)
    def _():
        def clear(i):
            acc[pl.ds(i, 8), :] = jnp.zeros((8, acc.shape[1]), F32)

        tiles(acc.shape[0], 8, clear)

    grad = g[...]
    for w, k, u_off, u_count in (
        (wl, cl, -halo, halo), (wo, co, 0, blk), (wr, cr, blk, halo),
    ):
        wide = up_to(u_count, 128) + 128
        piece[:, :u_count] = w[...] * dot_nt(grad, k[...])
        if piece.shape[1] > u_count:
            rest = piece.shape[1] - u_count
            piece[:, u_count:] = jnp.zeros((blk, rest), F32)

        def one_doc(d, first):
            last = first + len_ref[r, d]

            @pl.when((first < t0 + blk) & (last > t0))
            def _():
                low = jnp.clip(first - t0, 0, blk)
                high = jnp.clip(last - t0, 0, blk)
                col = padc + t0 + u_off - first
                col_base = pl.multiple_of((col // 128) * 128, 128)
                row = padr + t0 - first
                row_base = (row // 8) * 8

                def step(c, carry):
                    i0 = pl.multiple_of(c * size, size)
                    x = piece[pl.ds(i0, size), :wide]
                    t = t0 + i0 + lax.broadcasted_iota(jnp.int32, (size, wide), 0)
                    x = jnp.where((t >= first) & (t < last), x, 0.0)
                    x = pltpu.roll(x, col - col_base, 1)
                    x = jnp.concatenate([x, jnp.zeros((8, wide), F32)], axis=0)
                    x = pltpu.roll(x, row - row_base, 0)
                    at = (
                        pl.ds(pl.multiple_of(row_base + i0, 8), size + 8),
                        pl.ds(col_base, wide),
                    )
                    acc[at] += x
                    return carry

                lax.fori_loop(low // size, (high + size - 1) // size, step, 0)

            return last

        lax.fori_loop(0, docs, one_doc, jnp.int32(0))

    @pl.when(r == last_row)
    def _():
        for p in range(0, MAXDOC, 128):
            band[p : p + 128, :] = acc[
                padr + p : padr + p + 128, padc + p - WIN : padc + p - WIN + BAND
            ].astype(BF16)


def pair_outer(t0, lengths, weights, g, ce, blk, halo):
    rows, docs = lengths.shape
    d2 = g.shape[2]
    padr, padc = up_to(blk, 8), up_to(blk + halo, 128)
    most = up_to(max(blk, halo), 128) + 128
    blk3 = lambda *s: pl.BlockSpec((None,) + s, lambda r: (r,) + (0,) * len(s))
    return pl.pallas_call(
        partial(outer_kernel, (blk, halo, docs, padr, padc)),
        grid=(rows,),
        out_shape=jax.ShapeDtypeStruct((MAXDOC, BAND), BF16),
        in_specs=[
            pl.BlockSpec(memory_space=pltpu.SMEM),
            pl.BlockSpec(memory_space=pltpu.SMEM),
            blk3(blk, halo), blk3(blk, blk), blk3(blk, halo),
            blk3(blk, d2), blk3(halo, d2), blk3(blk, d2), blk3(halo, d2),
        ],
        out_specs=whole((MAXDOC, BAND)),
        scratch_shapes=[
            pltpu.VMEM((2 * padr + MAXDOC + 40, 2 * padc + MAXDOC + 128), F32),
            pltpu.VMEM((blk, most), F32),
        ],
        compiler_params=params(56),
        cost_estimate=cost(2 * rows * blk * (blk + 2 * halo) * d2, 14e6),
        name="outer",
    )(t0, lengths, *weights, g, *ce)


def entry_kernel(
    w2l, wo, w2r, gl, go, gr, k, v, q_grad, wq, wk, wv, x, res_grad, gain,
    in_grad, k_grad, v_grad, vectors, wt, acc,
):
    count, d = k.shape
    sub = min(32, count)
    halo = w2l.shape[0]

    @pl.when(pl.program_id(0) == 0)
    def _():
        vectors[...] = jnp.zeros_like(vectors)

    wt[:, 0:halo] = w2l[...].T.astype(BF16)
    wt[:, halo : halo + count] = wo[...].T.astype(BF16)
    wt[:, halo + count :] = w2r[...].T.astype(BF16)
    parts = (
        (slice(0, halo), gl), (slice(halo, halo + count), go),
        (slice(halo + count, 2 * halo + count), gr),
    )
    for n in range(0, d, 256):
        c, e = slice(n, n + 256), slice(d + n, d + n + 256)
        carried = sum(dot_nn(wt[:, s], g[:, c]) for s, g in parts)
        exps = sum(dot_nn(wt[:, s], g[:, e]) for s, g in parts)
        exp_key = jnp.exp(k[:, c].astype(F32))
        vg = (carried * exp_key).astype(BF16)
        kg = ((carried * v[:, c].astype(F32) + exps) * exp_key).astype(BF16)
        v_grad[:, c] = vg
        k_grad[:, c] = kg
        vectors[2:3, c] += jnp.sum(vg.astype(F32), axis=0, keepdims=True)
    qg, kg, vg = q_grad[...], k_grad[...], v_grad[...]
    for n in range(0, d, 256):
        c = slice(n, n + 256)
        acc[:, c] = dot_nt(qg, wq[c, :]) + dot_nt(kg, wk[c, :]) + dot_nt(vg, wv[c, :])

    def norm_tile(i):
        at = pl.ds(i, sub)
        unit, inverse = normalize(x[at, :].astype(F32))
        g = acc[at, :]
        in_grad[at, :] = res_grad[at, :] + norm_pull(g, unit, inverse, gain[...])
        vectors[0:1, :] += jnp.sum(g * unit, axis=0, keepdims=True)
        vectors[1:2, :] += jnp.sum(g, axis=0, keepdims=True)

    tiles(count, sub, norm_tile)


def entry(w2l, wo, w2r, gl, go, gr, k, v, q_grad, wq, wk, wv, x, res_grad, gain):
    rows, blk, d = k.shape
    halo = gl.shape[1]
    blk3 = lambda *s: pl.BlockSpec((None,) + s, lambda r: (r,) + (0,) * len(s))
    out = lambda t: jax.ShapeDtypeStruct((rows, blk, d), t)
    mat = whole((d, d))
    return pl.pallas_call(
        entry_kernel,
        grid=(rows,),
        out_shape=[out(F32), out(BF16), out(BF16), jax.ShapeDtypeStruct((8, d), F32)],
        in_specs=[
            blk3(halo, blk), blk3(blk, blk), blk3(halo, blk),
            blk3(halo, 2 * d), blk3(blk, 2 * d), blk3(halo, 2 * d),
            blk3(blk, d), blk3(blk, d), blk3(blk, d), mat, mat, mat,
            blk3(blk, d), blk3(blk, d), whole((1, d)),
        ],
        out_specs=[blk3(blk, d)] * 3 + [whole((8, d))],
        scratch_shapes=[pltpu.VMEM((blk, 2 * halo + blk), BF16), pltpu.VMEM((blk, d), F32)],
        compiler_params=params(56),
        cost_estimate=cost(5e9, 20e6),
        name="entry",
    )(w2l, wo, w2r, gl, go, gr, k, v, q_grad, wq, wk, wv, x, res_grad, gain)


def log2(n):
    return n.bit_length() - 1


def swap(value, axis, bit, n):
    return lax.ppermute(value, axis, [(i, i ^ (1 << bit)) for i in range(n)])


def halve(x, dim, axis, bit, n):
    me = (lax.axis_index(axis) >> bit) & 1
    send = lax.dynamic_index_in_dim(x, 1 - me, dim, keepdims=False).astype(BF16)
    keep = lax.dynamic_index_in_dim(x, me, dim, keepdims=False)
    return keep.astype(F32) + swap(send, axis, bit, n).astype(F32)


def reduce_shards(x, chans, row_ways, order):
    rows, cols = x.shape[1:]
    nc, nr = log2(chans), log2(row_ways)
    x = x.reshape((2,) * nc + (2,) * nr + (rows // row_ways, cols))
    dims = [("chan", b) for b in reversed(range(nc))] + [("rows", b) for b in reversed(range(nr))]
    steps = [("chan", 0)] + [("rows", b) for b in order] + [("chan", b) for b in range(1, nc)]
    for axis, bit in steps:
        dim = dims.index((axis, bit))
        x = halve(x, dim, axis, bit, chans if axis == "chan" else row_ways)
        dims.pop(dim)
    x = lax.optimization_barrier(x.astype(BF16))
    for bit in reversed(order):
        me = (lax.axis_index("rows") >> bit) & 1
        other = swap(x, "rows", bit, row_ways)
        dim = len([b for b in order[order.index(bit) + 1 :] if b > bit])
        x = jnp.stack([jnp.where(me == 0, x, other), jnp.where(me == 0, other, x)], axis=dim)
    return x.reshape(rows, cols)


def shift_tokens(value, by, n):
    return lax.ppermute(value, "chan", [(i, i + by) for i in range(n) if 0 <= i + by < n])


def window(value, reach, n):
    left = [shift_tokens(value, k, n) for k in range(reach, 0, -1)]
    right = [shift_tokens(value, -k, n) for k in range(1, reach + 1)]
    join = lambda parts: parts[0] if len(parts) == 1 else jnp.concatenate(parts, axis=1)
    return join(left), join(right)


def body(
    chans, row_ways,
    tokens, lengths, norm1_gain, norm1_bias, query_weight, query_offset_bias, key_weight,
    value_weight, value_offset_bias, output_weight, output_bias, norm2_gain, norm2_bias,
    raising_weight, raising_bias, lowering_weight, lowering_bias, pair_bias, out_cotangent,
):
    rows, blk, d = tokens.shape
    ff = raising_weight.shape[1]
    reach = -(-(WIN - 1) // blk)
    halo = reach * blk
    me = lax.axis_index("chan")
    t0 = (me * blk).astype(jnp.int32).reshape(1)
    one = lambda a: a.reshape(1, -1)
    flat = lambda a: a.reshape(-1, a.shape[-1])
    seq = lambda a: a.reshape(rows, -1, a.shape[-1])
    x_left, x_right = window(tokens, reach, chans)
    x = flat(tokens)
    cot = flat(out_cotangent)
    lead = (one(norm1_gain), one(norm1_bias), query_weight, one(query_offset_bias),
            key_weight, value_weight, one(value_offset_bias))
    wl, wo, wr, w2l, w2r = pair_weights(t0, lengths, pair_bias, blk, halo)
    normed, q, k, v, ce_own = project(x, *lead, True)
    ce_left = project(flat(x_left), *lead, False)
    ce_right = project(flat(x_right), *lead, False)
    ce = (seq(ce_left), seq(ce_own), seq(ce_right))
    mixed, ratio, den, resid, mid = mix(
        (wl, wo, wr), ce, seq(q), tokens, output_weight, one(output_bias),
        one(norm2_gain), one(norm2_bias),
    )
    block_out, mid_grad, dn_grad, up_grad, up_bias, dn_bias = feed(
        flat(mid), cot, flat(resid), raising_weight, one(raising_bias), lowering_weight,
        one(lowering_bias),
    )
    reduce = partial(reduce_shards, chans=chans, row_ways=row_ways)
    ways = list(range(log2(row_ways)))
    swung = ways[::-1]
    dn_total = reduce(dn_grad.reshape(chans, -1, d), order=ways)
    up_total = reduce(up_grad.reshape(chans, -1, ff), order=swung)
    res_grad, res_low, q_grad, pair, vec_mid = middle(
        mid_grad, flat(resid), cot, q, flat(ratio), flat(den), output_weight, one(norm2_gain)
    )
    g_left, g_right = window(seq(pair), reach, chans)
    shards = lambda a: a.astype(BF16).reshape(chans, -1, d)
    out_w = shards(dot_tn(flat(mixed), res_low))
    query_w = shards(dot_tn(normed, q_grad))
    band = pair_outer(t0, lengths, (wl, wo, wr), seq(pair), ce, blk, halo)
    early = reduce(jnp.concatenate([out_w, query_w], axis=1), order=ways)
    in_grad, k_grad, v_grad, vec_in = entry(
        w2l, wo, w2r, g_left, seq(pair), g_right, seq(k), seq(v), seq(q_grad),
        query_weight, key_weight, value_weight, tokens, seq(res_grad), one(norm1_gain),
    )
    key_w = shards(dot_tn(normed, flat(k_grad)))
    value_w = shards(dot_tn(normed, flat(v_grad)))
    small = [vec_in[0], vec_in[1], vec_mid[3], vec_in[2], vec_mid[2], vec_mid[0], vec_mid[1],
             dn_bias[0], up_bias[0]]
    packed = jnp.concatenate([a.reshape(chans, -1) for a in small], axis=1)
    share, lanes = MAXDOC // chans, d - BAND
    packed = jnp.pad(packed, ((0, 0), (0, share * lanes - packed.shape[1])))
    band = jnp.concatenate(
        [band.reshape(chans, share, BAND), packed.reshape(chans, share, lanes).astype(BF16)], axis=2
    )
    late = reduce(jnp.concatenate([key_w, value_w, band], axis=1), order=swung)
    part = d // chans
    tail = late[2 * part :].astype(F32)
    vectors = tail[:, BAND:].reshape(-1)
    sizes = [a.size // chans for a in small]
    outs, at = [], 0
    for n in sizes:
        outs.append(vectors[at : at + n])
        at += n
    gain1, shift1, query_b, value_b, out_b, gain2, shift2, dn_b, up_b = outs
    group = (me * share) // 128
    padded = jnp.pad(tail[:, :BAND], ((0, 0), (MAXDOC, MAXDOC)))
    pair_total = lax.dynamic_slice_in_dim(padded, MAXDOC + WIN - group * 128, MAXDOC, 1)
    f = lambda a: a.astype(F32)
    return (
        seq(block_out), in_grad, gain1, shift1, f(early[part:]), query_b, f(late[:part]),
        f(late[part : 2 * part]), value_b, f(early[:part]), out_b, gain2, shift2,
        f(up_total), up_b, f(dn_total), dn_b, pair_total,
    )


def solution(mesh):
    tokens = P("rows", "chan", None)
    vec, mat = P("chan"), P("chan", None)
    return jax.shard_map(
        partial(body, mesh.shape["chan"], mesh.shape["rows"]),
        mesh=mesh,
        in_specs=(tokens, P("rows", None)) + (P(),) * 16 + (tokens,),
        out_specs=(
            tokens, tokens, vec, vec, mat, vec, mat, mat, vec, mat, vec, vec, vec,
            mat, vec, mat, vec, mat,
        ),
        check_vma=False,
    )
```
